512 devices in a mesh: gx: 32 (over z, core), gy: 16 (over y, x).
Axes of the slice: x: 4, y: 4, z: 16, core: 2. Of those that a mesh axis runs over, the one named last changes fastest.
Arguments:
- tokens: bfloat16 [8192, 2048], P('gx'), may hold values from -6 to 6
- lengths: int32 [4], replicated, may hold values from 1 to 4096, 8192 in all
- adapter_of_request: int32 [4], replicated, may hold values from 0 to 15
- adapter_storage_slot: int32 [16], replicated, may hold values from 0 to 15, each once
- page_cache_slot: int32 [1024], P('gx'), may hold values from 0 to 1023, as said below
- query_key_value_weight: bfloat16 [2048, 16, 384], P(None, 'gy'), may hold values from -4 to 4
- adapter_down_maps: bfloat16 [16, 2048, 48], P('gy'), may hold values from -0.125 to 0.125
- adapter_up_maps: bfloat16 [16, 3, 16, 16, 128], P(None, None, None, 'gy'), may hold values from -1.5 to 1.5
- query_norm_gain: float32 [16, 128], P('gy'), may hold values from 0.25 to 1.75
- key_norm_gain: float32 [16, 128], P('gy'), may hold values from 0.25 to 1.75
- output_weight: bfloat16 [16, 128, 2048], P('gy'), may hold values from -0.125 to 0.125
- post_norm_gain: float32 [2048], replicated, may hold values from 0.25 to 1.75
Outputs:
- mixed: bfloat16 [8192, 2048], P('gx')
- kv_cache: bfloat16 [1024, 8, 16, 256], P('gx', None, 'gy')
The draws below stay inside these ranges and needn't reach their ends.
Inputs may be any that keep to these rules, and one draw needn't show every extreme that they name: `page_cache_slot`: each slot appears once; the 32 pages of the tokens of one index of gx have exactly 1 slot among the 32 slots held by each index k of gx (slots k * 32 onward).
All inputs are finite; a program needn't handle non-finite values.
Results may differ from the reference program's by a relative error of at most 0.017.
Values may be sent and summed in bfloat16 or wider, within the bound.
No kernel may reach another device: no remote copies, remote signals or barrier semaphores. Data moves between devices by JAX's collectives and lax.ppermute only.
A program may use at most 64 MiB of HBM per device.

```python
import math
import jax
import jax.numpy as jnp
import numpy as np
from jax import lax

MODEL_WIDTH = 2048
ATTENTION_HEADS = 16
HEAD_SIZE = 128
ADAPTER_RANK = 16
PAGE = 8
REQS = 4
ADAPTER_COUNT = 16
TOKENS = 8192
LONGEST = 4096
PAGES = 1024
PAGES_DEV = 32
PER_PEER = 1


def draw_tokens(key, part):
    drawn = jnp.clip(jax.random.normal(jax.random.fold_in(key, 11), (TOKENS, MODEL_WIDTH), jnp.float32), -6.0, 6.0)
    return drawn.astype(jnp.bfloat16)


def draw_query_key_value_weight(key, part):
    drawn = jnp.clip(jax.random.normal(jax.random.fold_in(key, 23), (MODEL_WIDTH, ATTENTION_HEADS, 3 * HEAD_SIZE), jnp.float32), -6.0, 6.0) * MODEL_WIDTH ** (-0.5)
    return drawn.astype(jnp.bfloat16)


def gain_table(key, salt):
    return jnp.clip(1.0 + 0.15 * jax.random.normal(jax.random.fold_in(key, salt), (ATTENTION_HEADS, HEAD_SIZE), jnp.float32), 0.25, 1.75)


def draw_query_norm_gain(key, part):
    return gain_table(key, 41)


def draw_key_norm_gain(key, part):
    return gain_table(key, 53)


def draw_page_cache_slot(key, part):
    groups = PAGES // PAGES_DEV
    first_key, second_key = jax.random.split(key)
    source_perm = jax.vmap(lambda sub: jax.random.permutation(sub, PAGES_DEV))(jax.random.split(first_key, groups))
    owner = source_perm // PER_PEER
    within = source_perm % PER_PEER
    target_perm = jax.vmap(lambda sub: jax.random.permutation(sub, PAGES_DEV))(jax.random.split(second_key, groups))
    source = jnp.arange(groups)[:, None]
    inner = target_perm[owner, source * PER_PEER + within]
    return (owner * PAGES_DEV + inner).reshape(PAGES).astype(jnp.int32)


def set_ends(array, rng, smallest, high):
    index_at = [jax.random.randint(jax.random.fold_in(rng, axis), (), 0, length) for axis, length in enumerate(array.shape)]
    longest = array.shape.index(max(array.shape))
    neighbour = index_at[:longest] + [(index_at[longest] + 1) % array.shape[longest]] + index_at[longest + 1:]
    return array.at[tuple(index_at)].set(smallest).at[tuple(neighbour)].set(high)


def level_of(stream_key, dims, pieces, smallest, high):
    def one(position, blocks):
        steps = jax.random.uniform(jax.random.fold_in(jax.random.fold_in(stream_key, 6), position), (blocks,), jnp.float32, smallest / len(pieces), high / len(pieces))
        return jnp.repeat(jnp.exp(steps), dims[position] // blocks).reshape((-1,) + (1,) * (len(dims) - position - 1))

    level = one(*pieces[0])
    for cut in pieces[1:]:
        level = level * one(*cut)
    return level


def cumulative_ranks(count, skew):
    loads = [(1 << 20) // math.isqrt(grade ** skew) + 1 for grade in range(1, count + 1)]
    spread = 1 + sum(loads) // (1 << 30)
    return np.cumsum(np.array([max(1, weight // spread) for weight in loads]))


def ranked(key, shape, count, slope):
    listing = cumulative_ranks(count, slope)
    ticket = jax.random.randint(jax.random.fold_in(key, 1), shape, 0, int(listing[count - 1]))
    standing = jnp.searchsorted(jnp.asarray(listing, jnp.int32), ticket, side="right")
    return jax.random.permutation(jax.random.fold_in(key, 2), count)[standing].astype(jnp.int32)


def profile(amount, total, bound, skew):
    loads = [(1 << 20) // math.isqrt(standing ** skew) + 1 for standing in range(2, amount + 1)]
    spare, counts = total - bound - (amount - 1), [1] * (amount - 1)
    while spare > 0:
        candidates = [i for i in range(amount - 1) if counts[i] < bound]
        pool, remaining = sum([loads[i] for i in candidates]), spare
        for i in candidates:
            more = min(bound - counts[i], max(1, remaining * loads[i] // pool), spare)
            counts[i] = counts[i] + more
            spare = spare - more
    return np.array([bound] + counts)


def uneven(rng, amount, total, most, slope):
    if amount == 2:
        one = jax.random.randint(rng, (), max(1, total - most), min(most, total - 1) + 1)
        return jnp.stack([one, total - one])
    sizes = jnp.asarray(profile(amount, total, most, slope), jnp.int32)
    pairs = (amount - 1) // 2
    donor, receiver = sizes[1:1 + 2 * pairs:2], sizes[2:2 + 2 * pairs:2]
    margin = jnp.minimum(donor - 1, most - receiver)
    passed = jax.random.randint(jax.random.fold_in(rng, 1), (pairs,), 0, 1 << 20) % (margin + 1)
    sizes = sizes.at[1:1 + 2 * pairs:2].set(donor - passed).at[2:2 + 2 * pairs:2].set(receiver + passed)
    return sizes[jax.random.permutation(jax.random.fold_in(rng, 2), amount)]


def bell_draw(own_key, extent, width, bound, cuts=(), dtype=jnp.bfloat16):
    result = width * jax.random.normal(own_key, extent, jnp.float32)
    if cuts:
        result = result * level_of(own_key, extent, cuts, -0.22, 0.18)
    return jnp.clip(result, -bound, bound).astype(dtype)


def setup_inputs(seed: int = 0) -> dict:
    arg_keys = jax.random.split(jax.random.key(seed), 13)
    return {
        "tokens": draw_tokens(jax.random.fold_in(arg_keys[12], 71), 0),
        "lengths": uneven(arg_keys[1], REQS, TOKENS, LONGEST, 2).astype(jnp.int32),
        "adapter_of_request": set_ends(ranked(arg_keys[2], (REQS,), ADAPTER_COUNT, 2), jax.random.fold_in(arg_keys[2], 3), 0, ADAPTER_COUNT - 1).astype(jnp.int32),
        "adapter_storage_slot": jax.random.permutation(arg_keys[3], ADAPTER_COUNT).astype(jnp.int32),
        "page_cache_slot": draw_page_cache_slot(jax.random.fold_in(arg_keys[12], 71), 0),
        "query_key_value_weight": draw_query_key_value_weight(jax.random.fold_in(arg_keys[12], 71), 0),
        "adapter_down_maps": bell_draw(arg_keys[6], (ADAPTER_COUNT, MODEL_WIDTH, 3 * ADAPTER_RANK), MODEL_WIDTH ** -0.5, 0.125, ((0, 16),)),
        "adapter_up_maps": bell_draw(arg_keys[7], (ADAPTER_COUNT, 3, ADAPTER_RANK, ATTENTION_HEADS, HEAD_SIZE), ADAPTER_RANK ** -0.5, 1.5, ((3, 16),)),
        "query_norm_gain": draw_query_norm_gain(jax.random.fold_in(arg_keys[12], 71), 0),
        "key_norm_gain": draw_key_norm_gain(jax.random.fold_in(arg_keys[12], 71), 0),
        "output_weight": bell_draw(arg_keys[10], (ATTENTION_HEADS, HEAD_SIZE, MODEL_WIDTH), MODEL_WIDTH ** -0.5, 0.125, ((0, 16),)),
        "post_norm_gain": jnp.clip(1.0 + 0.15 * jax.random.normal(arg_keys[11], (MODEL_WIDTH,), jnp.float32), 0.25, 1.75),
    }


def rotate(values, positions):
    half = values.shape[-1] // 2
    freq = 500000.0 ** (-(jnp.arange(half).astype(jnp.float32) * 2.0) / values.shape[-1])
    angle = positions.astype(jnp.float32)[:, None] * freq[None, :]
    cosine = jnp.cos(angle)[:, None, :]
    sine = jnp.sin(angle)[:, None, :]
    first = values[..., :half]
    second = values[..., half:]
    return jnp.concatenate([first * cosine - second * sine, second * cosine + first * sine], axis=-1)

def reference(tokens, lengths, adapter_of_request, adapter_storage_slot, page_cache_slot, query_key_value_weight, adapter_down_maps, adapter_up_maps, query_norm_gain, key_norm_gain, output_weight, post_norm_gain):
    count = tokens.shape[0]
    rows = jnp.arange(count).astype(jnp.int32)
    ends = jnp.cumsum(lengths).astype(jnp.int32)
    starts = ends - lengths
    request = lax.optimization_barrier(jnp.sum((ends[None, :] <= rows[:, None]).astype(jnp.int32), axis=1)).astype(jnp.int32)
    positions = rows - starts[request]
    slots = adapter_storage_slot[adapter_of_request[request]]
    onehot = (slots[:, None] == jnp.arange(ADAPTER_COUNT)[None, :]).astype(jnp.float32)
    reduced_rows = jnp.einsum('zm,ump->zup', tokens.astype(jnp.float32), adapter_down_maps.astype(jnp.float32))
    low = lax.optimization_barrier(jnp.sum(onehot[:, :, None] * reduced_rows, axis=1)).astype(jnp.bfloat16)
    expanded_rows = onehot[:, :, None, None] * low.astype(jnp.float32).reshape(count, 1, 3, ADAPTER_RANK)
    adapter_update = jnp.einsum('dzqi,zqibj->dqbj', expanded_rows, adapter_up_maps.astype(jnp.float32))
    base = jnp.einsum('td,dhe->the', tokens.astype(jnp.float32), query_key_value_weight.astype(jnp.float32))
    query = base[..., :HEAD_SIZE] + adapter_update[:, 0]
    key_raw = base[..., HEAD_SIZE:2 * HEAD_SIZE] + adapter_update[:, 1]
    value = base[..., 2 * HEAD_SIZE:] + adapter_update[:, 2]
    query_n = query * lax.rsqrt(lax.optimization_barrier(jnp.mean(query * query, axis=(1, 2))) + 1e-06)[:, None, None] * query_norm_gain[None]
    key_n = key_raw * lax.rsqrt(lax.optimization_barrier(jnp.mean(key_raw * key_raw, axis=(1, 2))) + 1e-06)[:, None, None] * key_norm_gain[None]
    query_b = rotate(query_n, positions).astype(jnp.bfloat16)
    key_b = rotate(key_n, positions).astype(jnp.bfloat16)
    value_b = value.astype(jnp.bfloat16)
    pages = jnp.concatenate([key_b, value_b], axis=-1).reshape(PAGES, PAGE, ATTENTION_HEADS, 2 * HEAD_SIZE)
    kv_cache = jnp.zeros_like(pages).at[page_cache_slot].set(pages)
    allowed = (request[:, None] == request[None, :]) & (rows[None, :] <= rows[:, None])
    scale = HEAD_SIZE ** (-0.5)

    def one_head(head):
        qh = query_b[:, head].astype(jnp.float32)
        kh = key_b[:, head].astype(jnp.float32)
        vh = value_b[:, head]
        scores = jnp.dot(qh, kh.T, precision=lax.Precision.HIGHEST) * scale
        masked = jnp.where(allowed, scores, -1e+30)
        best = lax.optimization_barrier(jnp.max(masked, axis=1))
        weights = jnp.where(allowed, jnp.exp(scores - best[:, None]), 0.0)
        total = lax.optimization_barrier(jnp.sum(weights, axis=1))
        weights_b = weights.astype(jnp.bfloat16)
        return jnp.dot(weights_b, vh, preferred_element_type=jnp.float32) / total[:, None]
    attn = lax.map(one_head, jnp.arange(ATTENTION_HEADS)).astype(jnp.bfloat16)
    output = jnp.einsum('hte,hed->td', attn.astype(jnp.float32), output_weight.astype(jnp.float32))
    normed = output * lax.rsqrt(lax.optimization_barrier(jnp.mean(output * output, axis=1)) + 1e-06)[:, None] * post_norm_gain[None, :]
    mixed = (tokens.astype(jnp.float32) + normed).astype(jnp.bfloat16)
    return (mixed, kv_cache)
```

```python
import jax
import jax.numpy as jnp
from jax import lax
from jax.experimental import pallas as pl
from jax.experimental.pallas import tpu as pltpu
from jax.sharding import PartitionSpec as P

MODEL_WIDTH = 2048
HEADS = 16
HEAD = 128
RANK = 16
PAGE = 8
REQS = 4
ROWS = 256
CHIP_ROWS = 2 * ROWS
GROUPS = 32
PAGES_HERE = ROWS // PAGE
HOPS = 4
FAR = 5
CHIPS = GROUPS // 2
NEG = -1e30
FLOOR = -1e29
BIG = 1 << 30
SCORE_SCALE = 1.4426950408889634 * HEAD ** (-0.5)
F32 = jnp.float32
BF16 = jnp.bfloat16

VMEM = pl.BlockSpec(memory_space=pltpu.VMEM)
SMEM = pl.BlockSpec(memory_space=pltpu.SMEM)


def contract(a, b, dims, precision=None):
    return lax.dot_general(
        a, b, (((dims[0],), (dims[1],)), ((), ())), precision=precision, preferred_element_type=F32
    )


def chips_apart(distance):
    return [(i, i + 2 * distance) for i in range(GROUPS) if 0 <= i + 2 * distance < GROUPS]


SIBLING = [(i, i ^ 1) for i in range(GROUPS)]


def low_kernel(lengths, adapters, storage, tokens, down, out):
    rows = lax.axis_index("gx") * ROWS + lax.broadcasted_iota(jnp.int32, (1, ROWS), 1)
    member = lax.axis_index("gy")
    begin = jnp.int32(0)
    chosen = jnp.zeros((1, ROWS), F32)
    for r in range(REQS):
        end = begin + lengths[r]
        from_row = jnp.where(storage[adapters[r]] == member, begin, BIG)
        chosen = jnp.where((rows >= from_row) & (rows < end), 1.0, chosen)
        begin = end
    reduced = contract(down[...], tokens[...], (1, 1))
    low = jnp.where(chosen > 0.0, reduced, 0.0).astype(BF16)
    for j in range(HEADS):
        out[j] = low


def project_kernel(lengths, adapters, storage, base, lows, up, qkv, squares):
    rows = lax.axis_index("gx") * ROWS + lax.broadcasted_iota(jnp.int32, (1, ROWS), 1)
    low = lows[0].astype(F32)
    for j in range(1, HEADS):
        low = low + lows[j].astype(F32)
    inside = []
    slots = []
    begin = jnp.int32(0)
    for r in range(REQS):
        end = begin + lengths[r]
        inside.append((rows >= begin) & (rows < end))
        slots.append(storage[adapters[r]])
        begin = end
    ones = jnp.ones((8, HEAD), F32)
    totals = []
    for c in range(3):
        part = low[c * RANK : (c + 1) * RANK]
        spread = jnp.concatenate([jnp.where(hit, part, 0.0) for hit in inside], axis=0).astype(BF16)
        maps = jnp.concatenate([up[slot, c] for slot in slots], axis=0)
        cols = slice(c * HEAD, (c + 1) * HEAD)
        value = base[:, cols] + contract(spread, maps, (0, 0))
        qkv[:, cols] = value
        if c < 2:
            totals.append(contract(ones, value * value, (1, 1), lax.Precision.HIGHEST))
    line = lax.broadcasted_iota(jnp.int32, (8, ROWS), 0)
    both = jnp.where(line < 4, totals[0], totals[1])
    for j in range(HEADS):
        squares[j] = both


def rotate_kernel(qkv, squares, query_gain, key_gain, cosine, sine, query, keys_values):
    total = squares[0]
    for j in range(1, HEADS):
        total = total + squares[j]
    line = lax.broadcasted_iota(jnp.int32, (8, HEAD), 0)

    def rotated(cols, pick, gain):
        square = contract(total, jnp.where(line == pick, 1.0, 0.0), (0, 0), lax.Precision.HIGHEST)
        value = qkv[:, cols] * lax.rsqrt(square / MODEL_WIDTH + 1e-06) * gain[...]
        return value * cosine[...] + pltpu.roll(value, HEAD // 2, 1) * sine[...]

    query[...] = (rotated(slice(0, HEAD), 0, query_gain) * SCORE_SCALE).astype(BF16)
    keys_values[0:ROWS] = rotated(slice(HEAD, 2 * HEAD), 4, key_gain).astype(BF16)
    keys_values[ROWS : 2 * ROWS] = qkv[:, 2 * HEAD : 3 * HEAD].astype(BF16)


def attend(lengths, query, blocks, scores, query_chip, key_chip):
    core = lax.rem(lax.axis_index("gx"), 2)
    lane = lax.broadcasted_iota(jnp.int32, (1, CHIP_ROWS), 1)
    flip = jnp.where(lane < ROWS, lane, lane - CHIP_ROWS)
    rows = query_chip * CHIP_ROWS + jnp.where(core == 0, lane, flip + ROWS)
    begin = jnp.zeros((1, CHIP_ROWS), jnp.int32)
    run = jnp.int32(0)
    for r in range(REQS - 1):
        run = run + lengths[r]
        begin = jnp.where(rows >= run, run, begin)
    place = lax.broadcasted_iota(jnp.int32, (ROWS, CHIP_ROWS), 0)
    best = jnp.full((1, CHIP_ROWS), FLOOR, F32)
    for i, block in enumerate(blocks):
        first = (key_chip - i) * CHIP_ROWS + core * ROWS
        score = contract(block[0:ROWS], query, (1, 1))
        allowed = (place >= begin - first) & (place <= rows - first)
        score = jnp.where(allowed, score, NEG)
        scores[i] = score
        best = jnp.maximum(best, jnp.max(score, axis=0, keepdims=True))
    best = best.astype(BF16).astype(F32)
    total = jnp.zeros((1, CHIP_ROWS), F32)
    accum = jnp.zeros((HEAD, CHIP_ROWS), F32)
    for i, block in enumerate(blocks):
        weight = jnp.exp2(scores[i] - best)
        total = total + jnp.sum(weight, axis=0, keepdims=True)
        accum = accum + contract(block[ROWS : 2 * ROWS], weight.astype(BF16), (0, 0))
    return best, total, accum


def far_kernel(lengths, query, b0, b1, b2, b3, out, scores):
    chip = lax.axis_index("gx") // 2
    best, total, accum = attend(
        lengths, query[...], (b0, b1, b2, b3), scores, chip + FAR, chip
    )
    out[0:HEAD] = accum.astype(BF16)
    line = lax.broadcasted_iota(jnp.int32, (16, CHIP_ROWS), 0)
    high = total.astype(BF16).astype(F32)
    rest = jnp.where(line == 1, high, jnp.where(line == 2, total - high, 0.0))
    out[HEAD : HEAD + 16] = jnp.where(line == 0, best, rest).astype(BF16)


def near_kernel(lengths, query, b0, b1, b2, b3, b4, out, scores):
    chip = lax.axis_index("gx") // 2
    best, total, accum = attend(
        lengths, query[...], (b0, b1, b2, b3, b4), scores, chip, chip
    )
    out[0:HEAD] = accum
    line = lax.broadcasted_iota(jnp.int32, (8, CHIP_ROWS), 0)
    out[HEAD : HEAD + 8] = jnp.where(line == 0, best, total)


def merge_kernel(near, far, mine, theirs):
    chip = lax.axis_index("gx") // 2
    stats = far[HEAD : HEAD + 16].astype(F32)
    best_far = jnp.where(chip >= FAR, stats[0:1], FLOOR)
    total_far = stats[1:2] + stats[2:3]
    tail = near[HEAD : HEAD + 8]
    best_near = tail[0:1]
    best = jnp.maximum(best_near, best_far)
    a = jnp.exp2(best_near - best)
    b = jnp.exp2(best_far - best)
    accum = near[0:HEAD] * a + far[0:HEAD].astype(F32) * b
    total = tail[1:2] * a + total_far * b
    line = lax.broadcasted_iota(jnp.int32, (8, CHIP_ROWS), 0)
    stat = jnp.where(line == 0, best, total)
    mine[0:HEAD] = accum[:, 0:ROWS]
    mine[HEAD : HEAD + 8] = stat[:, 0:ROWS]
    theirs[0:HEAD] = accum[:, ROWS:CHIP_ROWS]
    theirs[HEAD : HEAD + 8] = stat[:, ROWS:CHIP_ROWS]


def finish_kernel(mine, other, out):
    s0 = mine[HEAD : HEAD + 8]
    s1 = other[HEAD : HEAD + 8]
    best = jnp.maximum(s0[0:1], s1[0:1])
    a = jnp.exp2(s0[0:1] - best)
    b = jnp.exp2(s1[0:1] - best)
    total = s0[1:2] * a + s1[1:2] * b
    attn = (mine[0:HEAD] * a + other[0:HEAD] * b) / total
    attn = attn.T.astype(BF16)
    for j in range(HEADS):
        out[j] = attn


TILE = 512


def output_kernel(attn, weight, tokens, gain, out, rows_attn, result, square):
    step = pl.program_id(0)

    @pl.when(step == 0)
    def _():
        for h in range(HEADS):
            rows_attn[:, h * HEAD : (h + 1) * HEAD] = attn[h]
        square[...] = jnp.zeros_like(square)

    part = jnp.dot(rows_attn[...], weight[...], preferred_element_type=F32)
    result[step] = part
    square[...] += jnp.sum(part * part, axis=1, keepdims=True)

    @pl.when(step == pl.num_programs(0) - 1)
    def _():
        scale = lax.rsqrt(square[...] / MODEL_WIDTH + 1e-06)
        for s in range(MODEL_WIDTH // TILE):
            cols = slice(s * TILE, (s + 1) * TILE)
            normed = result[s] * scale * gain[:, cols]
            out[:, cols] = (tokens[:, cols].astype(F32) + normed).astype(BF16)


def project_out(attn, weight, tokens, gain):
    whole = lambda shape: pl.BlockSpec(shape, lambda n: (0,) * len(shape))
    return pl.pallas_call(
        output_kernel,
        grid=(MODEL_WIDTH // TILE,),
        in_specs=[
            whole((HEADS, ROWS, HEAD)),
            pl.BlockSpec((MODEL_WIDTH, TILE), lambda n: (0, n)),
            whole((ROWS, MODEL_WIDTH)),
            whole((1, MODEL_WIDTH)),
        ],
        out_specs=whole((ROWS, MODEL_WIDTH)),
        out_shape=jax.ShapeDtypeStruct((ROWS, MODEL_WIDTH), BF16),
        scratch_shapes=[
            pltpu.VMEM((ROWS, MODEL_WIDTH), BF16),
            pltpu.VMEM((MODEL_WIDTH // TILE, ROWS, TILE), F32),
            pltpu.VMEM((ROWS, 1), F32),
        ],
        name="project_out",
    )(attn, weight, tokens, gain)


def local(kernel, name, scalars, arrays, outs, scratch=()):
    specs = [SMEM] * len(scalars) + [VMEM] * len(arrays)
    shapes = [jax.ShapeDtypeStruct(shape, dtype) for shape, dtype in outs]
    single = len(shapes) == 1
    return pl.pallas_call(
        kernel,
        in_specs=specs,
        out_specs=VMEM if single else [VMEM] * len(shapes),
        out_shape=shapes[0] if single else shapes,
        scratch_shapes=list(scratch),
        name=name,
    )(*scalars, *arrays)


def exchange(copies):
    return lax.all_to_all(copies, "gy", split_axis=0, concat_axis=0, tiled=True)


def angles(lengths):
    rows = lax.axis_index("gx") * ROWS + jnp.arange(ROWS)
    begin = jnp.zeros((ROWS,), jnp.int32)
    run = jnp.int32(0)
    for r in range(REQS - 1):
        run = run + lengths[r]
        begin = jnp.where(rows >= run, run, begin)
    half = HEAD // 2
    freq = 500000.0 ** (-(jnp.arange(half).astype(F32) * 2.0) / HEAD)
    angle = (rows - begin).astype(F32)[:, None] * freq[None, :]
    cosine = jnp.cos(angle)
    sine = jnp.sin(angle)
    return jnp.concatenate([cosine, cosine], axis=1), jnp.concatenate([-sine, sine], axis=1)


def store_pages(keys_values, page_cache_slot):
    token = jnp.arange(ROWS)
    slot_of_token = jnp.repeat(page_cache_slot, PAGE)
    owner = slot_of_token // PAGES_HERE
    inner = (slot_of_token % PAGES_HERE).astype(BF16)
    goes_to = owner * PAGE + token % PAGE
    pick = (goes_to[None, :] == token[:, None]).astype(BF16)
    block = jnp.concatenate(
        [
            keys_values[0:ROWS],
            keys_values[ROWS : 2 * ROWS],
            jnp.broadcast_to(inner[:, None], (ROWS, HEAD)),
        ],
        axis=1,
    )
    sent = jnp.dot(pick, block, preferred_element_type=F32).astype(BF16)
    got = lax.all_to_all(
        sent.reshape(GROUPS, PAGE, 3 * HEAD), "gx", split_axis=0, concat_axis=0, tiled=True
    ).reshape(ROWS, 3 * HEAD)
    place = got[:, 2 * HEAD].astype(jnp.int32) * PAGE + token % PAGE
    put = (place[:, None] == token[None, :]).astype(BF16)
    stored = contract(put, got[:, 0 : 2 * HEAD], (0, 0)).astype(BF16)
    return stored.reshape(PAGES_HERE, PAGE, 1, 2 * HEAD)


def shards(
    tokens,
    lengths,
    adapter_of_request,
    adapter_storage_slot,
    page_cache_slot,
    query_key_value_weight,
    adapter_down_maps,
    adapter_up_maps,
    query_norm_gain,
    key_norm_gain,
    output_weight,
    post_norm_gain,
):
    whole_weight = lax.all_gather(output_weight[0], "gy", axis=0, tiled=True)
    scalars = (lengths, adapter_of_request, adapter_storage_slot)
    lows = local(
        low_kernel,
        "low",
        scalars,
        (tokens, jnp.swapaxes(adapter_down_maps[0], 0, 1)),
        [((HEADS, 3 * RANK, ROWS), BF16)],
    )
    lows = exchange(lows)
    base = jnp.dot(tokens, query_key_value_weight[:, 0], preferred_element_type=F32)
    cosine, sine = angles(lengths)
    qkv, squares = local(
        project_kernel,
        "project",
        scalars,
        (base, lows, adapter_up_maps[:, :, :, 0]),
        [((ROWS, 3 * HEAD), F32), ((HEADS, 8, ROWS), F32)],
    )
    squares = exchange(squares)
    query, block = local(
        rotate_kernel,
        "rotate",
        (),
        (qkv, squares, query_norm_gain, key_norm_gain, cosine, sine),
        [((ROWS, HEAD), BF16), ((2 * ROWS, HEAD), BF16)],
    )
    blocks = [block]
    for _ in range(HOPS):
        blocks.append(lax.ppermute(blocks[-1], "gx", chips_apart(1)))
    sibling = lax.ppermute(query, "gx", SIBLING)
    queries = jnp.concatenate([query, sibling], axis=0)
    far_queries = lax.ppermute(queries, "gx", chips_apart(-FAR))
    far = local(
        far_kernel,
        "attend_far",
        (lengths,),
        (far_queries, *blocks[:HOPS]),
        [((HEAD + 16, CHIP_ROWS), BF16)],
        [pltpu.VMEM((HOPS, ROWS, CHIP_ROWS), F32)],
    )
    far = lax.ppermute(far, "gx", chips_apart(FAR))
    near = local(
        near_kernel,
        "attend_near",
        (lengths,),
        (queries, *blocks),
        [((HEAD + 8, CHIP_ROWS), F32)],
        [pltpu.VMEM((HOPS + 1, ROWS, CHIP_ROWS), F32)],
    )
    mine, theirs = local(
        merge_kernel,
        "merge",
        (),
        (near, far),
        [((HEAD + 8, ROWS), F32), ((HEAD + 8, ROWS), F32)],
    )
    other = lax.ppermute(theirs, "gx", SIBLING)
    attn = local(finish_kernel, "finish", (), (mine, other), [((HEADS, ROWS, HEAD), BF16)])
    attn = exchange(attn)
    mixed = project_out(attn, whole_weight, tokens, post_norm_gain[None, :])
    kv_cache = store_pages(block, page_cache_slot)
    return (mixed, kv_cache)


def solution(mesh):
    return jax.shard_map(
        shards,
        mesh=mesh,
        in_specs=(
            P("gx", None),
            P(),
            P(),
            P(),
            P("gx"),
            P(None, "gy", None),
            P("gy", None, None),
            P(None, None, None, "gy", None),
            P("gy", None),
            P("gy", None),
            P("gy", None, None),
            P(),
        ),
        out_specs=(P("gx", None), P("gx", None, "gy", None)),
        check_vma=False,
    )
```

```python
import jax
import jax.numpy as jnp
from jax import lax
from jax.experimental import pallas as pl
from jax.experimental.pallas import tpu as pltpu
from jax.sharding import PartitionSpec as P

MODEL_WIDTH = 2048
HEADS = 16
HEAD = 128
RANK = 16
PAGE = 8
REQS = 4
ROWS = 256
GROUPS = 32
REACH = 17
PAGES_HERE = ROWS // PAGE
WIDE = MODEL_WIDTH // 2
SIBLING = [(i, i ^ 1) for i in range(GROUPS)]
NEG = -1e30
FLOOR = -1e29
BIG = 1 << 30
SCORE_SCALE = 1.4426950408889634 * HEAD ** (-0.5)
F32 = jnp.float32
BF16 = jnp.bfloat16


def contract(a, b, dims, precision=None):
    return lax.dot_general(
        a, b, (((dims[0],), (dims[1],)), ((), ())), precision=precision, preferred_element_type=F32
    )


def iota(shape, axis):
    return lax.broadcasted_iota(jnp.int32, shape, axis)


def group():
    return lax.axis_index("gx")


def low_kernel(lengths, adapters, storage, tokens, down, out):
    rows = group() * ROWS + iota((1, ROWS), 1)
    member = lax.axis_index("gy")
    begin = jnp.int32(0)
    chosen = jnp.zeros((1, ROWS), F32)
    for r in range(REQS):
        end = begin + lengths[r]
        from_row = jnp.where(storage[adapters[r]] == member, begin, BIG)
        chosen = jnp.where((rows >= from_row) & (rows < end), 1.0, chosen)
        begin = end
    reduced = contract(down[...], tokens[...], (1, 1))
    low = jnp.where(chosen > 0.0, reduced, 0.0).astype(BF16)
    for j in range(HEADS):
        out[j] = low


def base_kernel(
    lengths, adapters, storage, tokens, weight, up, wide, base, maps, positions, dup, done
):
    core = lax.rem(group(), 2)
    half = pl.ds(pl.multiple_of(core * WIDE, WIDE), WIDE)
    copies = [pltpu.make_async_copy(wide.at[:, half], dup.at[j], done.at[j]) for j in range(HEADS)]
    for copy in copies:
        copy.start()
    rows = group() * ROWS + iota((ROWS, HEAD), 0)
    begin = jnp.zeros((ROWS, HEAD), jnp.int32)
    run = jnp.int32(0)
    for r in range(REQS - 1):
        run = run + lengths[r]
        begin = jnp.where(rows >= run, run, begin)
    positions[...] = (rows - begin).astype(F32)
    base[...] = jnp.dot(tokens[...], weight[...], preferred_element_type=F32)
    for r in range(REQS):
        slot = storage[adapters[r]]
        for c in range(3):
            maps[c, r * RANK : (r + 1) * RANK] = up[slot, c]
    for copy in copies:
        copy.wait()


def project_kernel(
    lengths, base, lows, maps, query_gain, key_gain, cosine, sine, query, keys_values, squares
):
    rows = group() * ROWS + iota((1, ROWS), 1)
    low = lows[0].astype(F32)
    for j in range(1, HEADS):
        low = low + lows[j].astype(F32)
    inside = []
    begin = jnp.int32(0)
    for r in range(REQS):
        end = begin + lengths[r]
        inside.append((rows >= begin) & (rows < end))
        begin = end
    ones = jnp.ones((8, HEAD), F32)
    values = []
    for c in range(3):
        part = low[c * RANK : (c + 1) * RANK]
        spread = jnp.concatenate([jnp.where(hit, part, 0.0) for hit in inside], axis=0).astype(BF16)
        cols = slice(c * HEAD, (c + 1) * HEAD)
        values.append(base[:, cols] + contract(spread, maps[c], (0, 0)))
    totals = [contract(ones, v * v, (1, 1), lax.Precision.HIGHEST) for v in values[:2]]
    both = jnp.where(iota((8, ROWS), 0) < 4, totals[0], totals[1])
    for j in range(HEADS):
        squares[j] = both

    def rotated(value, gain):
        value = value * gain[...]
        return value * cosine[...] + pltpu.roll(value, HEAD // 2, 1) * sine[...]

    query[...] = rotated(values[0], query_gain)
    keys_values[0:ROWS] = rotated(values[1], key_gain).astype(BF16)
    keys_values[ROWS : 2 * ROWS] = values[2].astype(BF16)


def column(line_values, pick):
    return line_values.T[:, pick : pick + 1]


def scale_kernel(raw, squares, slots, query, facts):
    total = squares[0]
    for j in range(1, HEADS):
        total = total + squares[j]
    factor = lax.rsqrt(total / MODEL_WIDTH + 1e-06)
    query[...] = (raw[...] * column(factor, 0) * SCORE_SCALE).astype(BF16)
    facts[...] = jnp.where(iota((8, ROWS), 0) == 0, slots[...].astype(F32), factor)


def normed_keys(blocks, factors):
    def one(i):
        return (blocks[i, 0:ROWS].astype(F32) * factors[:, i : i + 1]).astype(BF16)

    return one


def attend_kernel(lengths, query, facts, blocks, out, scores, held, done):
    me = group()
    first = jnp.clip(me - (REACH - 1), 0, GROUPS - REACH)
    copy = pltpu.make_async_copy(blocks.at[pl.ds(first, REACH)], held, done)
    copy.start()
    rows = me * ROWS + iota((1, ROWS), 1)
    begin = jnp.zeros((1, ROWS), jnp.int32)
    run = jnp.int32(0)
    for r in range(REQS - 1):
        run = run + lengths[r]
        begin = jnp.where(rows >= run, run, begin)
    place = iota((ROWS, ROWS), 0)
    factors = jnp.concatenate([facts[first + i, 4:5] for i in range(REACH)], axis=0).T
    key = normed_keys(held, factors)
    best = jnp.full((1, ROWS), FLOOR, F32)
    copy.wait()
    for i in range(REACH):
        score = contract(key(i), query[...], (1, 1))
        start = (first + i) * ROWS
        allowed = (place >= begin - start) & (place <= rows - start)
        score = jnp.where(allowed, score, NEG)
        scores[i] = score
        best = jnp.maximum(best, jnp.max(score, axis=0, keepdims=True))
    total = jnp.zeros((1, ROWS), F32)
    accum = jnp.zeros((HEAD, ROWS), F32)
    for i in range(REACH):
        weight = jnp.exp2(scores[i] - best)
        total = total + jnp.sum(weight, axis=0, keepdims=True)
        accum = accum + contract(held[i, ROWS : 2 * ROWS], weight.astype(BF16), (0, 0))
    attn = (accum / total).T.astype(BF16)
    for j in range(HEADS):
        out[j] = attn


def place_kernel(facts, blocks, cache, held, done):
    me = group()
    copy = pltpu.make_async_copy(blocks, held, done)
    copy.start()
    token = iota((1, ROWS), 1) & 7
    target = iota((ROWS, ROWS), 0)
    factors = jnp.concatenate([facts[i, 4:5] for i in range(GROUPS)], axis=0).T
    normed = normed_keys(held, factors)
    key = jnp.zeros((ROWS, HEAD), F32)
    value = jnp.zeros((ROWS, HEAD), F32)
    copy.wait()
    for i in range(GROUPS):
        slot = facts[i, 0:1].astype(jnp.int32)
        goes_to = jnp.where((slot >> 5) == me, (slot & 31) * PAGE + token, -1)
        pick = jnp.where(goes_to == target, 1.0, 0.0).astype(BF16)
        key = key + jnp.dot(pick, normed(i), preferred_element_type=F32)
        value = value + jnp.dot(pick, held[i, ROWS : 2 * ROWS], preferred_element_type=F32)
    cache[:, 0:HEAD] = key.astype(BF16)
    cache[:, HEAD : 2 * HEAD] = value.astype(BF16)


CHUNK = 512
AHEAD = 8


def output_kernel(attn, tokens, gain, mine, theirs, out, rows_attn, result, held, done):
    core = lax.rem(group(), 2)
    copies = []
    for side, weight in enumerate((mine, theirs)):
        for n in range(MODEL_WIDTH // CHUNK):
            rows = slice(n * CHUNK, (n + 1) * CHUNK)
            slot = done.at[side, n]
            copies.append(pltpu.make_async_copy(weight.at[rows], held.at[side, rows], slot))
    for copy in copies[:AHEAD]:
        copy.start()
    for h in range(HEADS):
        rows_attn[:, h * HEAD : (h + 1) * HEAD] = attn[h]
    square = jnp.zeros((ROWS, 1), F32)
    for side in range(2):
        for n in range(MODEL_WIDTH // CHUNK):
            rows = slice(n * CHUNK, (n + 1) * CHUNK)
            step = side * (MODEL_WIDTH // CHUNK) + n
            copies[step].wait()
            for copy in copies[step + AHEAD : step + AHEAD + 1]:
                copy.start()
            part = jnp.dot(rows_attn[:, rows], held[side, rows], preferred_element_type=F32)
            total = part if n == 0 else result[core ^ side] + part
            result[core ^ side] = total
        square = square + jnp.sum(total * total, axis=1, keepdims=True)
    scale = lax.rsqrt(square / MODEL_WIDTH + 1e-06)
    for s in range(2):
        cols = slice(s * WIDE, (s + 1) * WIDE)
        normed = result[s] * scale * gain[:, cols]
        out[:, cols] = (tokens[:, cols].astype(F32) + normed).astype(BF16)


def local(kernel, name, scalars, arrays, outs, scratch=(), stay=(), outside=()):
    specs = [pl.BlockSpec(memory_space=pltpu.SMEM)] * len(scalars)
    for n in range(len(arrays)):
        specs.append(pl.BlockSpec(memory_space=pltpu.HBM if n in stay else pltpu.VMEM))
    spaces = {True: pltpu.VMEM, False: pltpu.HBM}
    arrays = [pltpu.with_memory_space_constraint(a, spaces[near]) for near, a in arrays]
    scalars = [pltpu.with_memory_space_constraint(a, pltpu.HBM) for a in scalars]
    kinds = {True: pltpu.VMEM, False: jax.ShapeDtypeStruct, None: pltpu.HBM}
    shapes = [kinds[near](shape, dtype) for near, shape, dtype in outs]
    single = len(shapes) == 1
    out_specs = []
    for n in range(len(outs)):
        out_specs.append(pl.BlockSpec(memory_space=pltpu.HBM if n in outside else pltpu.VMEM))
    return pl.pallas_call(
        kernel,
        in_specs=specs,
        out_specs=out_specs[0] if single else out_specs,
        out_shape=shapes[0] if single else shapes,
        scratch_shapes=list(scratch),
        compiler_params=pltpu.CompilerParams(vmem_limit_bytes=16 << 20),
        name=name,
    )(*scalars, *arrays)


def exchange(copies, axis):
    return lax.all_to_all(copies, axis, split_axis=0, concat_axis=0, tiled=True)


def angles(positions):
    lane = jnp.arange(HEAD) % (HEAD // 2)
    freq = 500000.0 ** (-(lane.astype(F32) * 2.0) / HEAD)
    angle = positions * freq[None, :]
    sign = jnp.where(jnp.arange(HEAD) < HEAD // 2, -1.0, 1.0)
    return jnp.cos(angle), jnp.sin(angle) * sign[None, :]


def shards(
    tokens,
    lengths,
    adapter_of_request,
    adapter_storage_slot,
    page_cache_slot,
    query_key_value_weight,
    adapter_down_maps,
    adapter_up_maps,
    query_norm_gain,
    key_norm_gain,
    output_weight,
    post_norm_gain,
):
    together = lax.optimization_barrier
    gy = "gy"
    scalars = (lengths, adapter_of_request, adapter_storage_slot)
    lows = local(
        low_kernel,
        "low",
        scalars,
        ((False, tokens), (False, jnp.swapaxes(adapter_down_maps[0], 0, 1))),
        [(False, (HEADS, 3 * RANK, ROWS), BF16)],
    )
    lows = exchange(lows, gy)
    base, maps, positions, wide = local(
        base_kernel,
        "base",
        scalars,
        (
            (False, tokens),
            (False, query_key_value_weight[:, 0]),
            (False, adapter_up_maps[:, :, :, 0]),
            (False, output_weight[0]),
        ),
        [
            (True, (ROWS, 3 * HEAD), F32),
            (True, (3, REQS * RANK, HEAD), BF16),
            (True, (ROWS, HEAD), F32),
            (None, (HEADS, HEAD, WIDE), BF16),
        ],
        [pltpu.SemaphoreType.DMA((HEADS,))],
        (),
        (3,),
    )
    slots = jnp.repeat(page_cache_slot, PAGE)[None, :]
    cosine, sine = angles(positions)
    raw, block, squares = local(
        project_kernel,
        "project",
        scalars[:1],
        (
            (True, base),
            (True, lows),
            (True, maps),
            (False, query_norm_gain),
            (False, key_norm_gain),
            (True, cosine),
            (True, sine),
        ),
        [
            (False, (ROWS, HEAD), F32),
            (False, (2 * ROWS, HEAD), BF16),
            (False, (HEADS, 8, ROWS), F32),
        ],
    )
    blocks = lax.all_gather(block, "gx", axis=0, tiled=True).reshape(GROUPS, 2 * ROWS, HEAD)
    squares = exchange(squares, gy)
    query, facts = local(
        scale_kernel,
        "scale",
        (),
        ((True, raw), (True, squares), (True, slots)),
        [(True, (ROWS, HEAD), BF16), (True, (8, ROWS), F32)],
    )
    facts, wide = together((facts, wide))
    facts = lax.all_gather(facts, "gx", axis=0, tiled=True).reshape(GROUPS, 8, ROWS)
    mine = exchange(wide, gy).reshape(MODEL_WIDTH, WIDE)
    mine, facts = together((mine, facts))
    attn = local(
        attend_kernel,
        "attend",
        (lengths,),
        ((True, query), (True, facts), (False, blocks)),
        [(None, (HEADS, ROWS, HEAD), BF16)],
        [
            pltpu.VMEM((REACH, ROWS, ROWS), F32),
            pltpu.VMEM((REACH, 2 * ROWS, HEAD), BF16),
            pltpu.SemaphoreType.DMA,
        ],
        (2,),
    )
    attn = exchange(attn, gy)
    kv_cache = local(
        place_kernel,
        "place",
        (),
        ((True, facts), (False, blocks)),
        [(False, (ROWS, 2 * HEAD), BF16)],
        [pltpu.VMEM((GROUPS, 2 * ROWS, HEAD), BF16), pltpu.SemaphoreType.DMA],
        (1,),
    )
    theirs = lax.ppermute(mine, "gx", SIBLING)
    mixed = local(
        output_kernel,
        "project_out",
        (),
        (
            (True, attn),
            (True, tokens),
            (False, post_norm_gain[None, :]),
            (False, mine),
            (False, theirs),
        ),
        [(False, (ROWS, MODEL_WIDTH), BF16)],
        [
            pltpu.VMEM((ROWS, MODEL_WIDTH), BF16),
            pltpu.VMEM((2, ROWS, WIDE), F32),
            pltpu.VMEM((2, MODEL_WIDTH, WIDE), BF16),
            pltpu.SemaphoreType.DMA((2, MODEL_WIDTH // CHUNK)),
        ],
        (3, 4),
    )
    return (mixed, kv_cache.reshape(PAGES_HERE, PAGE, 1, 2 * HEAD))


def solution(mesh):
    return jax.shard_map(
        shards,
        mesh=mesh,
        in_specs=(
            P("gx", None),
            P(),
            P(),
            P(),
            P("gx"),
            P(None, "gy", None),
            P("gy", None, None),
            P(None, None, None, "gy", None),
            P("gy", None),
            P("gy", None),
            P("gy", None, None),
            P(),
        ),
        out_specs=(P("gx", None), P("gx", None, "gy", None)),
        check_vma=False,
    )
```

```python
import jax
import jax.numpy as jnp
from jax import lax
from jax.experimental import pallas as pl
from jax.experimental.pallas import tpu as pltpu
from jax.sharding import PartitionSpec as P

MODEL_WIDTH = 2048
HEADS = 16
HEAD = 128
RANK = 16
PAGE = 8
REQS = 4
ROWS = 256
GROUPS = 32
REACH = 17
FRONT = 5
PAGES_HERE = ROWS // PAGE
WIDE = MODEL_WIDTH // 2
SIBLING = [(i, i ^ 1) for i in range(GROUPS)]
NEG = -1e30
FLOOR = -1e29
BIG = 1 << 30
SCORE_SCALE = 1.4426950408889634 * HEAD ** (-0.5)
F32 = jnp.float32
BF16 = jnp.bfloat16


def contract(a, b, dims, precision=None):
    return lax.dot_general(
        a, b, (((dims[0],), (dims[1],)), ((), ())), precision=precision, preferred_element_type=F32
    )


def iota(shape, axis):
    return lax.broadcasted_iota(jnp.int32, shape, axis)


def group():
    return lax.axis_index("gx")


def low_kernel(lengths, adapters, storage, tokens, down, out):
    rows = group() * ROWS + iota((1, ROWS), 1)
    member = lax.axis_index("gy")
    begin = jnp.int32(0)
    chosen = jnp.zeros((1, ROWS), F32)
    for r in range(REQS):
        end = begin + lengths[r]
        from_row = jnp.where(storage[adapters[r]] == member, begin, BIG)
        chosen = jnp.where((rows >= from_row) & (rows < end), 1.0, chosen)
        begin = end
    reduced = contract(tokens[...], down[...], (1, 1)).T
    low = jnp.where(chosen > 0.0, reduced, 0.0).astype(BF16)
    for j in range(HEADS):
        out[j] = low


def base_kernel(
    lengths, adapters, storage, tokens, weight, up, wide, base, maps, positions, dup, done
):
    core = lax.rem(group(), 2)
    half = pl.ds(pl.multiple_of(core * WIDE, WIDE), WIDE)
    copies = [pltpu.make_async_copy(wide.at[:, half], dup.at[j], done.at[j]) for j in range(HEADS)]
    for copy in copies:
        copy.start()
    rows = group() * ROWS + iota((ROWS, HEAD), 0)
    begin = jnp.zeros((ROWS, HEAD), jnp.int32)
    run = jnp.int32(0)
    for r in range(REQS - 1):
        run = run + lengths[r]
        begin = jnp.where(rows >= run, run, begin)
    positions[...] = (rows - begin).astype(F32)
    base[...] = jnp.dot(tokens[...], weight[...], preferred_element_type=F32)
    for r in range(REQS):
        slot = storage[adapters[r]]
        for c in range(3):
            maps[c, r * RANK : (r + 1) * RANK] = up[slot, c]
    for copy in copies:
        copy.wait()


def updates(lengths, lows, maps, parts):
    rows = group() * ROWS + iota((1, ROWS), 1)
    first, last = min(parts) * RANK, (max(parts) + 1) * RANK
    low = lows[0, first:last].astype(F32)
    for j in range(1, HEADS):
        low = low + lows[j, first:last].astype(F32)
    inside = []
    begin = jnp.int32(0)
    for r in range(REQS):
        end = begin + lengths[r]
        inside.append((rows >= begin) & (rows < end))
        begin = end
    out = []
    for c in parts:
        part = low[c * RANK - first : (c + 1) * RANK - first]
        spread = jnp.concatenate([jnp.where(hit, part, 0.0) for hit in inside], axis=0).astype(BF16)
        out.append(contract(spread, maps[c], (0, 0)))
    return out


def rotated(value, gain, cosine, sine):
    value = value * gain[...]
    return value * cosine[...] + pltpu.roll(value, HEAD // 2, 1) * sine[...]


def keys_kernel(lengths, base, lows, maps, key_gain, cosine, sine, keys_values, key_raw):
    key, value = updates(lengths, lows, maps, (1, 2))
    key = key + base[:, HEAD : 2 * HEAD]
    value = value + base[:, 2 * HEAD : 3 * HEAD]
    key_raw[...] = key
    keys_values[0:ROWS] = rotated(key, key_gain, cosine, sine).astype(BF16)
    keys_values[ROWS : 2 * ROWS] = value.astype(BF16)


def query_kernel(lengths, base, lows, maps, query_gain, cosine, sine, key_raw, query, squares):
    (value,) = updates(lengths, lows, maps, (0,))
    value = value + base[:, 0:HEAD]
    ones = jnp.ones((8, HEAD), F32)
    key = key_raw[...]
    totals = [contract(ones, v * v, (1, 1), lax.Precision.HIGHEST) for v in (value, key)]
    both = jnp.where(iota((8, ROWS), 0) < 4, totals[0], totals[1])
    for j in range(HEADS):
        squares[j] = both
    query[...] = rotated(value, query_gain, cosine, sine)


def column(line_values, pick):
    return line_values.T[:, pick : pick + 1]


def scale_kernel(raw, squares, slots, query, facts):
    total = squares[0]
    for j in range(1, HEADS):
        total = total + squares[j]
    factor = lax.rsqrt(total / MODEL_WIDTH + 1e-06)
    query[...] = (raw[...] * column(factor, 0) * SCORE_SCALE).astype(BF16)
    facts[...] = jnp.where(iota((8, ROWS), 0) == 0, slots[...].astype(F32), factor)


def normed_keys(blocks, factors):
    def one(i):
        return (blocks[i, 0:ROWS].astype(F32) * factors[:, i : i + 1]).astype(BF16)

    return one


def attend_kernel(lengths, query, facts, blocks, out, scores, held, done):
    me = group()
    first = jnp.clip(me - (REACH - 1), 0, GROUPS - REACH)
    copies = []
    for n, (low, high) in enumerate(((0, FRONT), (FRONT, REACH))):
        source = blocks.at[pl.ds(first + low, high - low)]
        copies.append(pltpu.make_async_copy(source, held.at[low:high], done.at[n]))
        copies[n].start()
    rows = me * ROWS + iota((1, ROWS), 1)
    begin = jnp.zeros((1, ROWS), jnp.int32)
    run = jnp.int32(0)
    for r in range(REQS - 1):
        run = run + lengths[r]
        begin = jnp.where(rows >= run, run, begin)
    place = iota((ROWS, ROWS), 0)
    factors = jnp.concatenate([facts[first + i, 4:5] for i in range(REACH)], axis=0).T
    key = normed_keys(held, factors)
    best = jnp.full((1, ROWS), FLOOR, F32)
    copies[0].wait()
    for i in range(REACH):
        if i == FRONT:
            copies[1].wait()
        score = contract(key(i), query[...], (1, 1))
        start = (first + i) * ROWS
        allowed = (place >= begin - start) & (place <= rows - start)
        score = jnp.where(allowed, score, NEG)
        scores[i] = score
        best = jnp.maximum(best, jnp.max(score, axis=0, keepdims=True))
    total = jnp.zeros((1, ROWS), F32)
    accum = jnp.zeros((HEAD, ROWS), F32)
    for i in range(REACH):
        weight = jnp.exp2(scores[i] - best)
        total = total + jnp.sum(weight, axis=0, keepdims=True)
        accum = accum + contract(held[i, ROWS : 2 * ROWS], weight.astype(BF16), (0, 0))
    attn = (accum / total).T.astype(BF16)
    for j in range(HEADS):
        out[j] = attn


def place_kernel(facts, blocks, cache, held, done):
    me = group()
    copy = pltpu.make_async_copy(blocks, held, done)
    copy.start()
    token = iota((1, ROWS), 1) & 7
    target = iota((ROWS, ROWS), 0)
    factors = jnp.concatenate([facts[i, 4:5] for i in range(GROUPS)], axis=0).T
    normed = normed_keys(held, factors)
    key = jnp.zeros((ROWS, HEAD), F32)
    value = jnp.zeros((ROWS, HEAD), F32)
    copy.wait()
    for i in range(GROUPS):
        slot = facts[i, 0:1].astype(jnp.int32)
        goes_to = jnp.where((slot >> 5) == me, (slot & 31) * PAGE + token, -1)
        pick = jnp.where(goes_to == target, 1.0, 0.0).astype(BF16)
        key = key + jnp.dot(pick, normed(i), preferred_element_type=F32)
        value = value + jnp.dot(pick, held[i, ROWS : 2 * ROWS], preferred_element_type=F32)
    cache[:, 0:HEAD] = key.astype(BF16)
    cache[:, HEAD : 2 * HEAD] = value.astype(BF16)


CHUNK = 512
AHEAD = 8


def output_kernel(attn, tokens, gain, mine, theirs, out, rows_attn, result, held, done):
    core = lax.rem(group(), 2)
    copies = []
    for side, weight in enumerate((mine, theirs)):
        for n in range(MODEL_WIDTH // CHUNK):
            rows = slice(n * CHUNK, (n + 1) * CHUNK)
            slot = done.at[side, n]
            copies.append(pltpu.make_async_copy(weight.at[rows], held.at[side, rows], slot))
    for copy in copies[:AHEAD]:
        copy.start()
    for h in range(HEADS):
        rows_attn[:, h * HEAD : (h + 1) * HEAD] = attn[h]
    square = jnp.zeros((ROWS, 1), F32)
    for side in range(2):
        for n in range(MODEL_WIDTH // CHUNK):
            rows = slice(n * CHUNK, (n + 1) * CHUNK)
            step = side * (MODEL_WIDTH // CHUNK) + n
            copies[step].wait()
            for copy in copies[step + AHEAD : step + AHEAD + 1]:
                copy.start()
            part = jnp.dot(rows_attn[:, rows], held[side, rows], preferred_element_type=F32)
            total = part if n == 0 else result[core ^ side] + part
            result[core ^ side] = total
        square = square + jnp.sum(total * total, axis=1, keepdims=True)
    scale = lax.rsqrt(square / MODEL_WIDTH + 1e-06)
    for s in range(2):
        cols = slice(s * WIDE, (s + 1) * WIDE)
        normed = result[s] * scale * gain[:, cols]
        out[:, cols] = (tokens[:, cols].astype(F32) + normed).astype(BF16)


def local(kernel, name, scalars, arrays, outs, scratch=(), stay=(), outside=()):
    specs = [pl.BlockSpec(memory_space=pltpu.SMEM)] * len(scalars)
    for n in range(len(arrays)):
        specs.append(pl.BlockSpec(memory_space=pltpu.HBM if n in stay else pltpu.VMEM))
    spaces = {True: pltpu.VMEM, False: pltpu.HBM}
    arrays = [pltpu.with_memory_space_constraint(a, spaces[near]) for near, a in arrays]
    scalars = [pltpu.with_memory_space_constraint(a, pltpu.HBM) for a in scalars]
    kinds = {True: pltpu.VMEM, False: jax.ShapeDtypeStruct, None: pltpu.HBM}
    shapes = [kinds[near](shape, dtype) for near, shape, dtype in outs]
    single = len(shapes) == 1
    out_specs = []
    for n in range(len(outs)):
        out_specs.append(pl.BlockSpec(memory_space=pltpu.HBM if n in outside else pltpu.VMEM))
    return pl.pallas_call(
        kernel,
        in_specs=specs,
        out_specs=out_specs[0] if single else out_specs,
        out_shape=shapes[0] if single else shapes,
        scratch_shapes=list(scratch),
        compiler_params=pltpu.CompilerParams(vmem_limit_bytes=16 << 20),
        name=name,
    )(*scalars, *arrays)


def exchange(copies, axis):
    return lax.all_to_all(copies, axis, split_axis=0, concat_axis=0, tiled=True)


def angles(positions):
    lane = jnp.arange(HEAD) % (HEAD // 2)
    freq = 500000.0 ** (-(lane.astype(F32) * 2.0) / HEAD)
    angle = positions * freq[None, :]
    sign = jnp.where(jnp.arange(HEAD) < HEAD // 2, -1.0, 1.0)
    return jnp.cos(angle), jnp.sin(angle) * sign[None, :]


def shards(
    tokens,
    lengths,
    adapter_of_request,
    adapter_storage_slot,
    page_cache_slot,
    query_key_value_weight,
    adapter_down_maps,
    adapter_up_maps,
    query_norm_gain,
    key_norm_gain,
    output_weight,
    post_norm_gain,
):
    together = lax.optimization_barrier
    gy = "gy"
    scalars = (lengths, adapter_of_request, adapter_storage_slot)
    lows = local(
        low_kernel,
        "low",
        scalars,
        ((False, tokens), (False, jnp.swapaxes(adapter_down_maps[0], 0, 1))),
        [(False, (HEADS, 3 * RANK, ROWS), BF16)],
    )
    lows = exchange(lows, gy)
    base, maps, positions, wide = local(
        base_kernel,
        "base",
        scalars,
        (
            (False, tokens),
            (False, query_key_value_weight[:, 0]),
            (False, adapter_up_maps[:, :, :, 0]),
            (False, output_weight[0]),
        ),
        [
            (True, (ROWS, 3 * HEAD), F32),
            (True, (3, REQS * RANK, HEAD), BF16),
            (True, (ROWS, HEAD), F32),
            (None, (HEADS, HEAD, WIDE), BF16),
        ],
        [pltpu.SemaphoreType.DMA((HEADS,))],
        (),
        (3,),
    )
    slots = jnp.repeat(page_cache_slot, PAGE)[None, :]
    cosine, sine = angles(positions)
    block, key_raw = local(
        keys_kernel,
        "keys",
        scalars[:1],
        (
            (True, base),
            (True, lows),
            (True, maps),
            (False, key_norm_gain),
            (True, cosine),
            (True, sine),
        ),
        [(None, (2 * ROWS, HEAD), BF16), (True, (ROWS, HEAD), F32)],
    )
    raw, squares = local(
        query_kernel,
        "query",
        scalars[:1],
        (
            (True, base),
            (True, lows),
            (True, maps),
            (False, query_norm_gain),
            (True, cosine),
            (True, sine),
            (True, key_raw),
        ),
        [(False, (ROWS, HEAD), F32), (False, (HEADS, 8, ROWS), F32)],
    )
    blocks = lax.all_gather(block, "gx", axis=0, tiled=True).reshape(GROUPS, 2 * ROWS, HEAD)
    squares = exchange(squares, gy)
    query, facts = local(
        scale_kernel,
        "scale",
        (),
        ((True, raw), (True, squares), (True, slots)),
        [(True, (ROWS, HEAD), BF16), (True, (8, ROWS), F32)],
    )
    facts, wide = together((facts, wide))
    facts = lax.all_gather(facts, "gx", axis=0, tiled=True).reshape(GROUPS, 8, ROWS)
    mine = exchange(wide, gy).reshape(MODEL_WIDTH, WIDE)
    mine, facts = together((mine, facts))
    attn = local(
        attend_kernel,
        "attend",
        (lengths,),
        ((True, query), (True, facts), (False, blocks)),
        [(None, (HEADS, ROWS, HEAD), BF16)],
        [
            pltpu.VMEM((REACH, ROWS, ROWS), F32),
            pltpu.VMEM((REACH, 2 * ROWS, HEAD), BF16),
            pltpu.SemaphoreType.DMA((2,)),
        ],
        (2,),
    )
    mine, attn = together((mine, attn))
    attn = exchange(attn, gy)
    kv_cache = local(
        place_kernel,
        "place",
        (),
        ((True, facts), (False, blocks)),
        [(False, (ROWS, 2 * HEAD), BF16)],
        [pltpu.VMEM((GROUPS, 2 * ROWS, HEAD), BF16), pltpu.SemaphoreType.DMA],
        (1,),
    )
    theirs = lax.ppermute(mine, "gx", SIBLING)
    mixed = local(
        output_kernel,
        "project_out",
        (),
        (
            (True, attn),
            (True, tokens),
            (False, post_norm_gain[None, :]),
            (False, mine),
            (False, theirs),
        ),
        [(False, (ROWS, MODEL_WIDTH), BF16)],
        [
            pltpu.VMEM((ROWS, MODEL_WIDTH), BF16),
            pltpu.VMEM((2, ROWS, WIDE), F32),
            pltpu.VMEM((2, MODEL_WIDTH, WIDE), BF16),
            pltpu.SemaphoreType.DMA((2, MODEL_WIDTH // CHUNK)),
        ],
        (3, 4),
    )
    return (mixed, kv_cache.reshape(PAGES_HERE, PAGE, 1, 2 * HEAD))


def solution(mesh):
    return jax.shard_map(
        shards,
        mesh=mesh,
        in_specs=(
            P("gx", None),
            P(),
            P(),
            P(),
            P("gx"),
            P(None, "gy", None),
            P("gy", None, None),
            P(None, None, None, "gy", None),
            P("gy", None),
            P("gy", None),
            P("gy", None, None),
            P(),
        ),
        out_specs=(P("gx", None), P("gx", None, "gy", None)),
        check_vma=False,
    )
```

```python
import jax
import jax.numpy as jnp
from jax import lax
from jax.experimental import pallas as pl
from jax.experimental.pallas import tpu as pltpu
from jax.sharding import PartitionSpec as P

MODEL_WIDTH = 2048
HEADS = 16
HEAD = 128
RANK = 16
PAGE = 8
REQS = 4
ROWS = 256
GROUPS = 32
REACH = 17
FRONT = 5
PAGES_HERE = ROWS // PAGE
WIDE = MODEL_WIDTH // 2
SIBLING = [(i, i ^ 1) for i in range(GROUPS)]
NEG = -1e30
FLOOR = -1e29
BIG = 1 << 30
SCORE_SCALE = 1.4426950408889634 * HEAD ** (-0.5)
F32 = jnp.float32
BF16 = jnp.bfloat16


def contract(a, b, dims, precision=None):
    return lax.dot_general(
        a, b, (((dims[0],), (dims[1],)), ((), ())), precision=precision, preferred_element_type=F32
    )


def iota(shape, axis):
    return lax.broadcasted_iota(jnp.int32, shape, axis)


def group():
    return lax.axis_index("gx")


def low_kernel(lengths, adapters, storage, tokens, down, out):
    rows = group() * ROWS + iota((1, ROWS), 1)
    member = lax.axis_index("gy")
    begin = jnp.int32(0)
    chosen = jnp.zeros((1, ROWS), F32)
    for r in range(REQS):
        end = begin + lengths[r]
        from_row = jnp.where(storage[adapters[r]] == member, begin, BIG)
        chosen = jnp.where((rows >= from_row) & (rows < end), 1.0, chosen)
        begin = end
    reduced = contract(tokens[...], down[...], (1, 1)).T
    low = jnp.where(chosen > 0.0, reduced, 0.0).astype(BF16)
    for j in range(HEADS):
        out[j] = low


def base_kernel(
    lengths,
    adapters,
    storage,
    tokens,
    weight,
    up,
    wide,
    query_gain,
    key_gain,
    base,
    maps,
    positions,
    dup,
    bounds,
    gains,
    done,
):
    line = iota((8, ROWS), 0)
    limits = jnp.zeros((8, ROWS), jnp.int32)
    start = jnp.int32(0)
    for r in range(REQS):
        limits = jnp.where(line == r, start, limits)
        start = start + lengths[r]
        limits = jnp.where(line == REQS + r, start, limits)
    bounds[...] = limits
    gains[0:1] = query_gain[...]
    gains[1:2] = key_gain[...]
    core = lax.rem(group(), 2)
    half = pl.ds(pl.multiple_of(core * WIDE, WIDE), WIDE)
    copies = [pltpu.make_async_copy(wide.at[:, half], dup.at[j], done.at[j]) for j in range(HEADS)]
    for copy in copies:
        copy.start()
    rows = group() * ROWS + iota((ROWS, HEAD), 0)
    begin = jnp.zeros((ROWS, HEAD), jnp.int32)
    run = jnp.int32(0)
    for r in range(REQS - 1):
        run = run + lengths[r]
        begin = jnp.where(rows >= run, run, begin)
    positions[...] = (rows - begin).astype(F32)
    base[...] = jnp.dot(tokens[...], weight[...], preferred_element_type=F32)
    for r in range(REQS):
        slot = storage[adapters[r]]
        for c in range(3):
            maps[c, r * RANK : (r + 1) * RANK] = up[slot, c]
    for copy in copies:
        copy.wait()


def updates(bounds, lows, maps, parts):
    rows = group() * ROWS + iota((1, ROWS), 1)
    first, last = min(parts) * RANK, (max(parts) + 1) * RANK
    low = lows[0, first:last].astype(F32)
    for j in range(1, HEADS):
        low = low + lows[j, first:last].astype(F32)
    inside = []
    for r in range(REQS):
        begin, end = bounds[r : r + 1], bounds[REQS + r : REQS + r + 1]
        inside.append((rows >= begin) & (rows < end))
    out = []
    for c in parts:
        part = low[c * RANK - first : (c + 1) * RANK - first]
        spread = jnp.concatenate([jnp.where(hit, part, 0.0) for hit in inside], axis=0).astype(BF16)
        out.append(contract(spread, maps[c], (0, 0)))
    return out


def rotated(value, gain, cosine, sine):
    value = value * gain
    return value * cosine[...] + pltpu.roll(value, HEAD // 2, 1) * sine[...]


def keys_kernel(bounds, base, lows, maps, gains, cosine, sine, keys_values, key_raw):
    key, value = updates(bounds, lows, maps, (1, 2))
    key = key + base[:, HEAD : 2 * HEAD]
    value = value + base[:, 2 * HEAD : 3 * HEAD]
    key_raw[...] = key
    keys_values[0:ROWS] = rotated(key, gains[1:2], cosine, sine).astype(BF16)
    keys_values[ROWS : 2 * ROWS] = value.astype(BF16)


def query_kernel(bounds, base, lows, maps, gains, cosine, sine, key_raw, query, squares):
    (value,) = updates(bounds, lows, maps, (0,))
    value = value + base[:, 0:HEAD]
    ones = jnp.ones((8, HEAD), F32)
    key = key_raw[...]
    totals = [contract(ones, v * v, (1, 1), lax.Precision.HIGHEST) for v in (value, key)]
    both = jnp.where(iota((8, ROWS), 0) < 4, totals[0], totals[1])
    for j in range(HEADS):
        squares[j] = both
    query[...] = rotated(value, gains[0:1], cosine, sine)


def column(line_values, pick):
    return line_values.T[:, pick : pick + 1]


def scale_kernel(raw, squares, slots, query, facts):
    total = squares[0]
    for j in range(1, HEADS):
        total = total + squares[j]
    factor = lax.rsqrt(total / MODEL_WIDTH + 1e-06)
    query[...] = (raw[...] * column(factor, 0) * SCORE_SCALE).astype(BF16)
    facts[...] = jnp.where(iota((8, ROWS), 0) == 0, slots[...].astype(F32), factor)


def normed_keys(blocks, factors):
    def one(i):
        return (blocks[i, 0:ROWS].astype(F32) * factors[:, i : i + 1]).astype(BF16)

    return one


def attend_kernel(bounds, query, facts, blocks, out, scores, held, done):
    me = group()
    first = jnp.clip(me - (REACH - 1), 0, GROUPS - REACH)
    copies = []
    for n, (low, high) in enumerate(((0, FRONT), (FRONT, REACH))):
        source = blocks.at[pl.ds(first + low, high - low)]
        copies.append(pltpu.make_async_copy(source, held.at[low:high], done.at[n]))
        copies[n].start()
    rows = me * ROWS + iota((1, ROWS), 1)
    begin = jnp.zeros((1, ROWS), jnp.int32)
    for r in range(1, REQS):
        start = bounds[r : r + 1]
        begin = jnp.where(rows >= start, start, begin)
    place = iota((ROWS, ROWS), 0)
    factors = jnp.concatenate([facts[first + i, 4:5] for i in range(REACH)], axis=0).T
    key = normed_keys(held, factors)
    best = jnp.full((1, ROWS), FLOOR, F32)
    copies[0].wait()
    for i in range(REACH):
        if i == FRONT:
            copies[1].wait()
        score = contract(key(i), query[...], (1, 1))
        start = (first + i) * ROWS
        allowed = (place >= begin - start) & (place <= rows - start)
        score = jnp.where(allowed, score, NEG)
        scores[i] = score
        best = jnp.maximum(best, jnp.max(score, axis=0, keepdims=True))
    total = jnp.zeros((1, ROWS), F32)
    accum = jnp.zeros((HEAD, ROWS), F32)
    for i in range(REACH):
        weight = jnp.exp2(scores[i] - best)
        total = total + jnp.sum(weight, axis=0, keepdims=True)
        accum = accum + contract(held[i, ROWS : 2 * ROWS], weight.astype(BF16), (0, 0))
    attn = (accum / total).T.astype(BF16)
    for j in range(HEADS):
        out[j] = attn


def place_kernel(facts, blocks, cache, held, done):
    me = group()
    copy = pltpu.make_async_copy(blocks, held, done)
    copy.start()
    token = iota((1, ROWS), 1) & 7
    target = iota((ROWS, ROWS), 0)
    factors = jnp.concatenate([facts[i, 4:5] for i in range(GROUPS)], axis=0).T
    normed = normed_keys(held, factors)
    key = jnp.zeros((ROWS, HEAD), F32)
    value = jnp.zeros((ROWS, HEAD), F32)
    copy.wait()
    for i in range(GROUPS):
        slot = facts[i, 0:1].astype(jnp.int32)
        goes_to = jnp.where((slot >> 5) == me, (slot & 31) * PAGE + token, -1)
        pick = jnp.where(goes_to == target, 1.0, 0.0).astype(BF16)
        key = key + jnp.dot(pick, normed(i), preferred_element_type=F32)
        value = value + jnp.dot(pick, held[i, ROWS : 2 * ROWS], preferred_element_type=F32)
    cache[:, 0:HEAD] = key.astype(BF16)
    cache[:, HEAD : 2 * HEAD] = value.astype(BF16)


CHUNK = 512
AHEAD = 8


def output_kernel(attn, tokens, gain, mine, theirs, out, rows_attn, result, held, done):
    core = lax.rem(group(), 2)
    copies = []
    for side, weight in enumerate((mine, theirs)):
        for n in range(MODEL_WIDTH // CHUNK):
            rows = slice(n * CHUNK, (n + 1) * CHUNK)
            slot = done.at[side, n]
            copies.append(pltpu.make_async_copy(weight.at[rows], held.at[side, rows], slot))
    for copy in copies[:AHEAD]:
        copy.start()
    for h in range(HEADS):
        rows_attn[:, h * HEAD : (h + 1) * HEAD] = attn[h]
    square = jnp.zeros((ROWS, 1), F32)
    for side in range(2):
        for n in range(MODEL_WIDTH // CHUNK):
            rows = slice(n * CHUNK, (n + 1) * CHUNK)
            step = side * (MODEL_WIDTH // CHUNK) + n
            copies[step].wait()
            for copy in copies[step + AHEAD : step + AHEAD + 1]:
                copy.start()
            part = jnp.dot(rows_attn[:, rows], held[side, rows], preferred_element_type=F32)
            total = part if n == 0 else result[core ^ side] + part
            result[core ^ side] = total
        square = square + jnp.sum(total * total, axis=1, keepdims=True)
    scale = lax.rsqrt(square / MODEL_WIDTH + 1e-06)
    for s in range(2):
        cols = slice(s * WIDE, (s + 1) * WIDE)
        normed = result[s] * scale * gain[:, cols]
        out[:, cols] = (tokens[:, cols].astype(F32) + normed).astype(BF16)


def local(kernel, name, scalars, arrays, outs, scratch=(), stay=(), outside=()):
    specs = [pl.BlockSpec(memory_space=pltpu.SMEM)] * len(scalars)
    for n in range(len(arrays)):
        specs.append(pl.BlockSpec(memory_space=pltpu.HBM if n in stay else pltpu.VMEM))
    spaces = {True: pltpu.VMEM, False: pltpu.HBM}
    arrays = [pltpu.with_memory_space_constraint(a, spaces[near]) for near, a in arrays]
    scalars = [pltpu.with_memory_space_constraint(a, pltpu.HBM) for a in scalars]
    kinds = {True: pltpu.VMEM, False: jax.ShapeDtypeStruct, None: pltpu.HBM}
    shapes = [kinds[near](shape, dtype) for near, shape, dtype in outs]
    single = len(shapes) == 1
    out_specs = []
    for n in range(len(outs)):
        out_specs.append(pl.BlockSpec(memory_space=pltpu.HBM if n in outside else pltpu.VMEM))
    return pl.pallas_call(
        kernel,
        in_specs=specs,
        out_specs=out_specs[0] if single else out_specs,
        out_shape=shapes[0] if single else shapes,
        scratch_shapes=list(scratch),
        compiler_params=pltpu.CompilerParams(vmem_limit_bytes=16 << 20),
        name=name,
    )(*scalars, *arrays)


def exchange(copies, axis):
    return lax.all_to_all(copies, axis, split_axis=0, concat_axis=0, tiled=True)


def angles(positions):
    lane = jnp.arange(HEAD) % (HEAD // 2)
    freq = 500000.0 ** (-(lane.astype(F32) * 2.0) / HEAD)
    angle = positions * freq[None, :]
    sign = jnp.where(jnp.arange(HEAD) < HEAD // 2, -1.0, 1.0)
    return jnp.cos(angle), jnp.sin(angle) * sign[None, :]


def shards(
    tokens,
    lengths,
    adapter_of_request,
    adapter_storage_slot,
    page_cache_slot,
    query_key_value_weight,
    adapter_down_maps,
    adapter_up_maps,
    query_norm_gain,
    key_norm_gain,
    output_weight,
    post_norm_gain,
):
    together = lax.optimization_barrier
    gy = "gy"
    scalars = (lengths, adapter_of_request, adapter_storage_slot)
    lows = local(
        low_kernel,
        "low",
        scalars,
        ((False, tokens), (False, jnp.swapaxes(adapter_down_maps[0], 0, 1))),
        [(False, (HEADS, 3 * RANK, ROWS), BF16)],
    )
    lows = exchange(lows, gy)
    base, maps, positions, wide, bounds, gains = local(
        base_kernel,
        "base",
        scalars,
        (
            (False, tokens),
            (False, query_key_value_weight[:, 0]),
            (False, adapter_up_maps[:, :, :, 0]),
            (False, output_weight[0]),
            (False, query_norm_gain),
            (False, key_norm_gain),
        ),
        [
            (True, (ROWS, 3 * HEAD), F32),
            (True, (3, REQS * RANK, HEAD), BF16),
            (True, (ROWS, HEAD), F32),
            (None, (HEADS, HEAD, WIDE), BF16),
            (True, (8, ROWS), jnp.int32),
            (True, (2, HEAD), F32),
        ],
        [pltpu.SemaphoreType.DMA((HEADS,))],
        (),
        (3,),
    )
    slots = jnp.repeat(page_cache_slot, PAGE)[None, :]
    cosine, sine = angles(positions)
    block, key_raw = local(
        keys_kernel,
        "keys",
        (),
        (
            (True, bounds),
            (True, base),
            (True, lows),
            (True, maps),
            (True, gains),
            (True, cosine),
            (True, sine),
        ),
        [(None, (2 * ROWS, HEAD), BF16), (True, (ROWS, HEAD), F32)],
    )
    raw, squares = local(
        query_kernel,
        "query",
        (),
        (
            (True, bounds),
            (True, base),
            (True, lows),
            (True, maps),
            (True, gains),
            (True, cosine),
            (True, sine),
            (True, key_raw),
        ),
        [(False, (ROWS, HEAD), F32), (False, (HEADS, 8, ROWS), F32)],
    )
    blocks = lax.all_gather(block, "gx", axis=0, tiled=True).reshape(GROUPS, 2 * ROWS, HEAD)
    squares = exchange(squares, gy)
    query, facts = local(
        scale_kernel,
        "scale",
        (),
        ((True, raw), (True, squares), (True, slots)),
        [(True, (ROWS, HEAD), BF16), (True, (8, ROWS), F32)],
    )
    facts, wide = together((facts, wide))
    facts = lax.all_gather(facts, "gx", axis=0, tiled=True).reshape(GROUPS, 8, ROWS)
    mine = exchange(wide, gy).reshape(MODEL_WIDTH, WIDE)
    mine, facts = together((mine, facts))
    attn = local(
        attend_kernel,
        "attend",
        (),
        ((True, bounds), (True, query), (True, facts), (False, blocks)),
        [(None, (HEADS, ROWS, HEAD), BF16)],
        [
            pltpu.VMEM((REACH, ROWS, ROWS), F32),
            pltpu.VMEM((REACH, 2 * ROWS, HEAD), BF16),
            pltpu.SemaphoreType.DMA((2,)),
        ],
        (3,),
    )
    mine, attn = together((mine, attn))
    attn = exchange(attn, gy)
    kv_cache = local(
        place_kernel,
        "place",
        (),
        ((True, facts), (False, blocks)),
        [(False, (ROWS, 2 * HEAD), BF16)],
        [pltpu.VMEM((GROUPS, 2 * ROWS, HEAD), BF16), pltpu.SemaphoreType.DMA],
        (1,),
    )
    theirs = lax.ppermute(mine, "gx", SIBLING)
    mixed = local(
        output_kernel,
        "project_out",
        (),
        (
            (True, attn),
            (True, tokens),
            (True, post_norm_gain[None, :]),
            (False, mine),
            (False, theirs),
        ),
        [(False, (ROWS, MODEL_WIDTH), BF16)],
        [
            pltpu.VMEM((ROWS, MODEL_WIDTH), BF16),
            pltpu.VMEM((2, ROWS, WIDE), F32),
            pltpu.VMEM((2, MODEL_WIDTH, WIDE), BF16),
            pltpu.SemaphoreType.DMA((2, MODEL_WIDTH // CHUNK)),
        ],
        (3, 4),
    )
    return (mixed, kv_cache.reshape(PAGES_HERE, PAGE, 1, 2 * HEAD))


def solution(mesh):
    return jax.shard_map(
        shards,
        mesh=mesh,
        in_specs=(
            P("gx", None),
            P(),
            P(),
            P(),
            P("gx"),
            P(None, "gy", None),
            P("gy", None, None),
            P(None, None, None, "gy", None),
            P("gy", None),
            P("gy", None),
            P("gy", None, None),
            P(),
        ),
        out_specs=(P("gx", None), P("gx", None, "gy", None)),
        check_vma=False,
    )
```
